32 devices in a mesh: frames: 8 (over y, x, core), slabs: 4 (over z).
Axes of the slice: x: 2, y: 2, z: 4, core: 2. Of those that a mesh axis runs over, the one named last changes fastest.
Arguments:
- frame_pixels: float32 [64, 384, 1024], P('frames', 'slabs'), may hold values from -6 to 6
- bragg_mask: int32 [64, 384, 1024], P('frames', 'slabs'), may hold values 0 or 1
- interp: bfloat16 [4, 4096, 1024], P('slabs'), may hold values from -0.09375 to 0.09375
- block_list: int32 [64, 4, 96], P('frames', 'slabs'), may hold values from 0 to 1023, as said below
- owner_map: int32 [4, 1024], P('slabs'), may hold values from 0 to 1023, as said below
- mirror_pair: int32 [4, 128], P('slabs'), may hold values from 0 to 127, as said below
Outputs:
- merged: float32 [4, 1024, 1024], P('slabs', 'frames')
The draws below stay inside these ranges and needn't reach their ends.
Inputs may be any that keep to these rules, and one draw needn't show every extreme that they name: `block_list`: among the list entries of the frames of one frame group in one slab group, at most 192 name blocks whose position lies in one owner's range of 128 positions, and in every such set some owner receives exactly 192. `owner_map`: each row is a permutation of the block numbers. `mirror_pair`: each row is a permutation; the row of slab group s xor (2) is the inverse of the row of s, so pairs are mutual.
All inputs are finite; a program needn't handle non-finite values. No bound on the sum of `bragg_mask` on one device may be relied on, other than what follows from the above.
Results may differ from the reference program's by a relative error of at most 0.0029.
Values may be sent and summed in bfloat16 or wider, within the bound.
No kernel may reach another device: no remote copies, remote signals or barrier semaphores. Data moves between devices by JAX's collectives and lax.ppermute only.
A program may use at most 128 MiB of HBM per device.

```python
import jax
import jax.numpy as jnp
from jax import lax

FRAME_DEV = 8
ROWS = 384
COLS = 1024
PANEL_ROWS = 4
RADIUS = 4
VOXELS = 1024
OWN_BLOCKS = 128
GROUPS = 8
SLABS = 4
FRAMES = 64
PANELS = 96
SLAB_BLOCKS = 1024
CAPACITY = 192


def block_table(key):
    table_rows = []
    for slab_index in range(SLABS):
        table_rows.append(jax.random.permutation(jax.random.fold_in(key, 100 + slab_index), SLAB_BLOCKS))
    return jnp.stack(table_rows).astype(jnp.int32)


def draw_owner_map(key, part):
    block_of = block_table(key)
    return jnp.argsort(block_of, axis=1).astype(jnp.int32)


def device_positions(device_key):
    key_slots = jax.random.fold_in(device_key, 1)
    key_favored = jax.random.fold_in(device_key, 2)
    key_shuffle = jax.random.fold_in(device_key, 3)
    key_within = jax.random.fold_in(device_key, 4)
    entry_count = FRAME_DEV * PANELS
    slots_all = jax.random.permutation(key_slots, GROUPS * CAPACITY)
    favored = jax.random.randint(key_favored, (), 0, GROUPS)
    priority = jnp.where(slots_all // CAPACITY == favored, 0, 1)
    sort_order = jnp.argsort(priority, stable=True)
    chosen = slots_all[sort_order][:entry_count]
    chosen = jax.random.permutation(key_shuffle, chosen)
    owner_index = chosen // CAPACITY
    slot_index = jax.random.randint(key_within, (entry_count,), 0, OWN_BLOCKS)
    return (owner_index * OWN_BLOCKS + slot_index).astype(jnp.int32)


def draw_block_list(key, part):
    block_of = block_table(key)
    device_keys = jax.random.split(jax.random.fold_in(key, 7), GROUPS * SLABS)
    positions = jax.vmap(device_positions)(device_keys)
    positions = positions.reshape(GROUPS, SLABS, FRAME_DEV * PANELS)
    slab_ids = jnp.arange(SLABS)[None, :, None]
    blocks = block_of[slab_ids, positions]
    blocks = blocks.reshape(GROUPS, SLABS, FRAME_DEV, PANELS)
    blocks = jnp.transpose(blocks, (0, 2, 1, 3)).reshape(FRAMES, SLABS, PANELS)
    return blocks.astype(jnp.int32)


def draw_mirror_pair(key, part):
    half_count = SLABS // 2
    table_rows = []
    for slab_index in range(SLABS):
        if slab_index < half_count:
            table_rows.append(jax.random.permutation(jax.random.fold_in(key, 300 + slab_index), OWN_BLOCKS))
        else:
            base_perm = jax.random.permutation(jax.random.fold_in(key, 300 + slab_index - half_count), OWN_BLOCKS)
            table_rows.append(jnp.argsort(base_perm))
    return jnp.stack(table_rows).astype(jnp.int32)


def place_ends(drawn, key, least, largest):
    place = [jax.random.randint(jax.random.fold_in(key, axis), (), 0, length) for axis, length in enumerate(drawn.shape)]
    longest = drawn.shape.index(max(drawn.shape))
    neighbour = place[:longest] + [(place[longest] + 1) % drawn.shape[longest]] + place[longest + 1:]
    return drawn.at[tuple(place)].set(least).at[tuple(neighbour)].set(largest)


def block_scale(stream_key, shape, pieces, least, largest):
    def one(axis_at, parts):
        heights = jax.random.uniform(jax.random.fold_in(jax.random.fold_in(stream_key, 6), axis_at), (parts,), jnp.float32, least / len(pieces), largest / len(pieces))
        return jnp.repeat(jnp.exp(heights), shape[axis_at] // parts).reshape((-1,) + (1,) * (len(shape) - axis_at - 1))

    loudness = one(*pieces[0])
    for cut in pieces[1:]:
        loudness = loudness * one(*cut)
    return loudness


def gaussian(own_key, shape, spread, most, shards=(), dtype=jnp.bfloat16):
    gain = block_scale(own_key, shape, shards, -0.22, 0.18) if shards else 1.0
    entries = jax.random.normal(own_key, shape, jnp.float32) * spread * gain
    return jnp.minimum(jnp.maximum(entries, -most), most).astype(dtype)


def setup_inputs(seed: int = 0) -> dict:
    seeds = jax.random.split(jax.random.key(seed), 7)
    frame_pixels = gaussian(seeds[0], (FRAMES, ROWS, COLS), 1.0, 6.0, ((0, 8), (1, 4)), jnp.float32)
    bragg_mask = place_ends((jax.random.randint(seeds[1], (FRAMES, ROWS, COLS), 0, 8) < 1).astype(jnp.int32), jax.random.fold_in(seeds[1], 1), 0, 1)
    interp = gaussian(seeds[2], (SLABS, PANEL_ROWS * COLS, VOXELS), (PANEL_ROWS * COLS) ** -0.5, 0.09375, ((0, 4),))
    block_list = draw_block_list(jax.random.fold_in(seeds[6], 71), 0)
    owner_map = draw_owner_map(jax.random.fold_in(seeds[6], 71), 0)
    mirror_pair = draw_mirror_pair(jax.random.fold_in(seeds[6], 71), 0)
    return {"frame_pixels": frame_pixels, "bragg_mask": bragg_mask, "interp": interp, "block_list": block_list, "owner_map": owner_map, "mirror_pair": mirror_pair}


EPSILON = 1e-05

def box_total(padded, row_count, col_count):
    box_width = 2 * RADIUS + 1
    row_sums = padded[:, 0:row_count, :]
    for offset in range(1, box_width):
        row_sums = row_sums + padded[:, offset:offset + row_count, :]
    full_sums = row_sums[:, :, 0:col_count]
    for offset in range(1, box_width):
        full_sums = full_sums + row_sums[:, :, offset:offset + col_count]
    return full_sums

def normalize(pixels, mask, row_padded):
    row_count = pixels.shape[1]
    col_count = pixels.shape[2]
    padded = jnp.pad(row_padded, ((0, 0), (0, 0), (RADIUS, RADIUS)))
    plain_sums = box_total(padded, row_count, col_count)
    square_sums = box_total(padded * padded, row_count, col_count)
    box_area = (2 * RADIUS + 1) * (2 * RADIUS + 1)
    box_mean = plain_sums / box_area
    box_var = square_sums / box_area - box_mean * box_mean
    scaled = (pixels - box_mean) * lax.rsqrt(box_var + EPSILON)
    return jnp.where(mask == 1, jnp.zeros_like(scaled), scaled).astype(jnp.bfloat16)

def reference(frame_pixels, bragg_mask, interp, block_list, owner_map, mirror_pair):
    weights_all = interp.astype(jnp.float32)
    pixel_groups = frame_pixels.reshape(GROUPS, FRAME_DEV, ROWS, COLS)
    mask_groups = bragg_mask.reshape(GROUPS, FRAME_DEV, ROWS, COLS)
    list_groups = block_list.reshape(GROUPS, FRAME_DEV, SLABS, PANELS)

    def accumulate(totals, inputs):
        pixels, mask, listed = inputs
        row_padded = jnp.pad(pixels, ((0, 0), (RADIUS, RADIUS), (0, 0)))
        corrected = normalize(pixels, mask, row_padded)
        panel_values = corrected.reshape(FRAME_DEV * PANELS, PANEL_ROWS * COLS).astype(jnp.float32)
        updated = []
        for slab_index in range(SLABS):
            terms = jnp.dot(panel_values, weights_all[slab_index], preferred_element_type=jnp.float32)
            position = owner_map[slab_index][listed[:, slab_index, :].reshape(-1)]
            added = jax.ops.segment_sum(terms, position, num_segments=SLAB_BLOCKS)
            updated.append(totals[slab_index] + added)
        return (jnp.stack(updated), None)
    start_sums = jnp.zeros((SLABS, SLAB_BLOCKS, VOXELS), jnp.float32)
    sums, _ = lax.scan(accumulate, start_sums, (pixel_groups, mask_groups, list_groups))
    half_count = SLABS // 2
    results = []
    for slab_index in range(SLABS):
        own_part = sums[slab_index].reshape(GROUPS, OWN_BLOCKS, VOXELS)
        partner = sums[slab_index ^ half_count].reshape(GROUPS, OWN_BLOCKS, VOXELS)
        paired = partner[:, mirror_pair[slab_index], :][:, :, ::-1]
        results.append((0.5 * (own_part + paired)).reshape(SLAB_BLOCKS, VOXELS))
    return jnp.stack(results)
```

```python
import functools

import jax
import jax.numpy as jnp
from jax import lax
from jax.experimental import pallas as pl
from jax.experimental.pallas import tpu as pltpu
from jax.sharding import PartitionSpec as P

PANEL_ROWS = 4
RADIUS = 4
EPSILON = 1e-05
LANES = 128


def swap(cells, axis, bit):
    count = lax.axis_size(axis)
    return lax.ppermute(cells, axis, [(i, i ^ bit) for i in range(count)])


def normalize_kernel(pixel_ref, mask_ref, top_ref, bottom_ref, out_ref, ext, plain, square, flat):
    frames, rows, cols = pixel_ref.shape
    ext_rows = rows + 2 * RADIUS
    wide = cols + LANES
    area = (2 * RADIUS + 1) ** 2
    plain[:, cols:] = jnp.zeros((rows, LANES), jnp.float32)
    square[:, cols:] = jnp.zeros((rows, LANES), jnp.float32)

    def down(x):
        two = x + pltpu.roll(x, ext_rows - 1, 0)
        four = two + pltpu.roll(two, ext_rows - 2, 0)
        eight = four + pltpu.roll(four, ext_rows - 4, 0)
        return eight[:rows] + x[2 * RADIUS :]

    def across(x):
        three = x + pltpu.roll(x, 1, 1) + pltpu.roll(x, wide - 1, 1)
        return (three + pltpu.roll(three, 3, 1) + pltpu.roll(three, wide - 3, 1))[:, :cols]

    for f in range(frames):
        ext[0:RADIUS] = top_ref[f]
        ext[RADIUS : RADIUS + rows] = pixel_ref[f]
        ext[RADIUS + rows :] = bottom_ref[f]
        for strip in range(cols // LANES):
            at = slice(strip * LANES, (strip + 1) * LANES)
            x = ext[:, at]
            plain[:, at] = down(x)
            square[:, at] = down(x * x)

        def strip_rows(i, carry):
            at = pl.ds(pl.multiple_of(i * 8, 8), 8)
            mean = across(plain[at, :]) * (1.0 / area)
            var = jnp.maximum(across(square[at, :]) * (1.0 / area) - mean * mean, 0.0)
            scaled = (pixel_ref[f, at, :] - mean) * lax.rsqrt(var + EPSILON)
            kept = jnp.where(mask_ref[f, at, :] == 1, 0.0, scaled)
            to = pl.ds(pl.multiple_of(f * rows + i * 8, 8), 8)
            for strip in range(cols // LANES):
                flat[strip, to, :] = kept[:, strip * LANES : (strip + 1) * LANES]
            return carry

        lax.fori_loop(0, rows // 8, strip_rows, 0, unroll=2)
    panels = frames * rows // PANEL_ROWS
    for r in range(PANEL_ROWS):
        for strip in range(cols // LANES):
            at = r * cols + strip * LANES
            out_ref[:, at : at + LANES] = flat[strip, pl.ds(r, panels, stride=PANEL_ROWS), :].astype(jnp.bfloat16)


def normalize(pixels, mask, top, bottom, first, count, step):
    _, rows, cols = pixels.shape
    block = step * rows // PANEL_ROWS
    base = first // step
    at = lambda i: (base + i, 0, 0)
    return pl.pallas_call(
        normalize_kernel,
        grid=(count // step,),
        in_specs=[
            pl.BlockSpec((step, rows, cols), at),
            pl.BlockSpec((step, rows, cols), at),
            pl.BlockSpec((step, RADIUS, cols), at),
            pl.BlockSpec((step, RADIUS, cols), at),
        ],
        out_specs=pl.BlockSpec((block, PANEL_ROWS * cols), lambda i: (i, 0)),
        out_shape=jax.ShapeDtypeStruct((count * rows // PANEL_ROWS, PANEL_ROWS * cols), jnp.bfloat16),
        scratch_shapes=[
            pltpu.VMEM((rows + 2 * RADIUS, cols), jnp.float32),
            pltpu.VMEM((rows, cols + LANES), jnp.float32),
            pltpu.VMEM((rows, cols + LANES), jnp.float32),
            pltpu.VMEM((cols // LANES, step * rows, LANES), jnp.float32),
        ],
        cost_estimate=pl.CostEstimate(flops=60 * count * rows * cols, bytes_accessed=10 * count * rows * cols, transcendentals=count * rows * cols),
        name="normalize",
    )(pixels, mask, top, bottom)


def anti_identity(n):
    a = lax.broadcasted_iota(jnp.int32, (n, n), 0)
    b = lax.broadcasted_iota(jnp.int32, (n, n), 1)
    return jnp.where(a + b == n - 1, 1.0, 0.0).astype(jnp.bfloat16)


def reversed_kernel(at_ref, w_ref, *outs):
    n = len(outs)
    width = outs[0].shape[1]
    flip = anti_identity(width)
    for j, out in enumerate(outs):
        k = n - 1 - j
        out[...] = jnp.dot(w_ref[:, k * width : (k + 1) * width], flip, preferred_element_type=jnp.float32).astype(jnp.bfloat16)


def reversed_share(weights, chip, other, chips, chunks):
    depth, voxels = weights.shape
    rows = depth // chips
    half = voxels // 2
    out = jax.ShapeDtypeStruct((rows, half // chunks), jnp.bfloat16)
    spec = pl.BlockSpec((rows, half // chunks), lambda i, at: (0, 0))
    return pl.pallas_call(
        reversed_kernel,
        grid_spec=pltpu.PrefetchScalarGridSpec(
            num_scalar_prefetch=1,
            grid=(1,),
            in_specs=[pl.BlockSpec((rows, half), lambda i, at: (at[0], at[1]))],
            out_specs=[spec] * chunks,
        ),
        out_shape=[out] * chunks,
        cost_estimate=pl.CostEstimate(flops=rows * half * half, bytes_accessed=4 * rows * half, transcendentals=0),
        name="reversed_share",
    )(jnp.stack([chip, other]).astype(jnp.int32), weights)


def position_kernel(own, list_ref, table_ref, mirror_ref, out_ref):
    entries = list_ref.shape[1]
    blocks = table_ref.shape[1]
    hot = (lax.broadcasted_iota(jnp.int32, (blocks, entries), 0) == list_ref[...]).astype(jnp.float32).astype(jnp.bfloat16)
    found = jnp.dot(table_ref[...].astype(jnp.float32).astype(jnp.bfloat16), hot, preferred_element_type=jnp.float32).astype(jnp.int32)
    owner = found[0:1]
    slot = found[1:2]
    hot_slot = (lax.broadcasted_iota(jnp.int32, (own, entries), 0) == slot).astype(jnp.float32).astype(jnp.bfloat16)
    mirrored = jnp.dot(mirror_ref[...].astype(jnp.float32).astype(jnp.bfloat16), hot_slot, preferred_element_type=jnp.float32).astype(jnp.int32)
    out_ref[0:1] = owner * own + slot
    out_ref[1:2] = owner * own + mirrored[0:1]


def positions(listed, owner_row, mirror_row):
    own = mirror_row.shape[0]
    blocks = owner_row.shape[0]
    entries = listed.shape[1]
    rows = lax.broadcasted_iota(jnp.int32, (8, blocks), 0)
    table = jnp.where(rows == 0, owner_row[None] // own, owner_row[None] % own)
    mirror = jnp.broadcast_to(mirror_row[None], (8, own))
    return pl.pallas_call(
        functools.partial(position_kernel, own),
        out_shape=jax.ShapeDtypeStruct((2, entries), jnp.int32),
        name="positions",
    )(listed, table, mirror)


def add_rows(pos, product, blocks):
    hot = (lax.broadcasted_iota(jnp.int32, (blocks, pos.shape[1]), 0) == pos).astype(jnp.float32).astype(jnp.bfloat16)
    high = product.astype(jnp.bfloat16)
    low = (product - high.astype(jnp.float32)).astype(jnp.bfloat16)
    return jnp.dot(hot, high, preferred_element_type=jnp.float32) + jnp.dot(hot, low, preferred_element_type=jnp.float32)


def own_kernel(count, has_sum, half_ref, *refs):
    xs = refs[:count]
    pos_ref, w_ref = refs[count : count + 2]
    out_ref, product = refs[-2:]
    row = 0
    for x in xs:
        n = x.shape[0]
        product[row : row + n] = jnp.dot(x[...], w_ref[...], preferred_element_type=jnp.float32)
        row += n
    total = add_rows(pos_ref[...], product[...], out_ref.shape[0])
    if has_sum:
        total = total + refs[count + 2][...]
    out_ref[...] = total


def own_products(xs, pos, weights, core, blocks, chunks, before=None):
    depth, voxels = weights.shape
    half = voxels // 2
    width = half // chunks
    rows = sum(x.shape[0] for x in xs)
    whole = lambda a: pl.BlockSpec(a.shape, lambda j, h: (0, 0))
    out_spec = pl.BlockSpec((blocks, width), lambda j, h: (0, j))
    in_specs = [whole(x) for x in xs] + [whole(pos), pl.BlockSpec((depth, width), lambda j, h: (0, h[0] * chunks + j))]
    args = list(xs) + [pos, weights]
    if before is not None:
        in_specs.append(out_spec)
        args.append(before)
    return pl.pallas_call(
        functools.partial(own_kernel, len(xs), before is not None),
        grid_spec=pltpu.PrefetchScalarGridSpec(
            num_scalar_prefetch=1,
            grid=(chunks,),
            in_specs=in_specs,
            out_specs=out_spec,
            scratch_shapes=[pltpu.VMEM((rows, width), jnp.float32)],
        ),
        out_shape=jax.ShapeDtypeStruct((blocks, half), jnp.float32),
        cost_estimate=pl.CostEstimate(flops=2 * rows * half * (depth + 2 * blocks), bytes_accessed=2 * depth * (rows + half) + 4 * blocks * half, transcendentals=0),
        name="own_products",
    )(core[None].astype(jnp.int32), *args)


def partner_kernel(count, pieces, at_ref, *refs):
    xs = refs[:count]
    pos_ref = refs[count]
    ws = refs[count + 1 : count + 1 + pieces]
    before_ref = refs[count + 1 + pieces]
    out_ref, product = refs[-2:]
    row = 0
    for x in xs:
        n = x.shape[0]
        acc = None
        for k, w in enumerate(ws):
            depth = w.shape[0]
            at = pl.ds(pl.multiple_of(at_ref[k], 128), depth)
            term = jnp.dot(x[:, at], w[...], preferred_element_type=jnp.float32)
            acc = term if acc is None else acc + term
        product[row : row + n] = acc
        row += n
    total = add_rows(pos_ref[...], product[...], out_ref.shape[0]) + before_ref[...]
    out_ref[...] = (0.5 * total).astype(jnp.bfloat16)


def partner_products(xs, pos, pieces, offsets, before, chunk):
    blocks, half = before.shape
    width = pieces[0].shape[1]
    depth = xs[0].shape[1]
    rows = sum(x.shape[0] for x in xs)
    whole = lambda a: pl.BlockSpec(a.shape, lambda i, at: (0, 0))
    return pl.pallas_call(
        functools.partial(partner_kernel, len(xs), len(pieces)),
        grid_spec=pltpu.PrefetchScalarGridSpec(
            num_scalar_prefetch=1,
            grid=(1,),
            in_specs=[whole(x) for x in xs] + [whole(pos)] + [whole(w) for w in pieces] + [pl.BlockSpec((blocks, width), lambda i, at: (0, chunk))],
            out_specs=pl.BlockSpec((blocks, width), lambda i, at: (0, 0)),
            scratch_shapes=[pltpu.VMEM((rows, width), jnp.float32)],
        ),
        out_shape=jax.ShapeDtypeStruct((blocks, width), jnp.bfloat16),
        cost_estimate=pl.CostEstimate(flops=2 * rows * width * (depth + 2 * blocks), bytes_accessed=2 * depth * (rows + width) + 6 * blocks * width, transcendentals=0),
        name="partner_products",
    )(offsets.astype(jnp.int32), *xs, pos, *pieces, before)


def merge_kernel(chunks, mirror_ref, *refs):
    owned = refs[:chunks]
    other = refs[chunks : 2 * chunks]
    out_ref = refs[-1]
    _, rows, width = owned[0].shape
    half = width * chunks
    flip = anti_identity(width)
    pick = (lax.broadcasted_iota(jnp.int32, (rows, rows), 1) == mirror_ref[...]).astype(jnp.float32).astype(jnp.bfloat16)
    for h in range(2):
        for j in range(chunks):
            turned = jnp.dot(other[chunks - 1 - j][1 - h], flip, preferred_element_type=jnp.float32).astype(jnp.bfloat16)
            paired = jnp.dot(pick, turned, preferred_element_type=jnp.float32)
            at = h * half + j * width
            out_ref[:, at : at + width] = owned[j][h] + paired


def merge(owned, other, mirror_col):
    _, rows, width = owned[0].shape
    return pl.pallas_call(
        functools.partial(merge_kernel, len(owned)),
        out_shape=jax.ShapeDtypeStruct((rows, 2 * width * len(owned)), jnp.float32),
        name="merge",
    )(mirror_col, *owned, *other)


def shards(frame_pixels, bragg_mask, interp, block_list, owner_map, mirror_pair):
    slab = lax.axis_index("slabs")
    member = lax.axis_index("frames")
    members = lax.axis_size("frames")
    slabs = lax.axis_size("slabs")
    assert slabs == 4 and members % 2 == 0
    chips = members // 2
    core = member % 2
    chip = member // 2
    chunks = 2
    frames, rows, cols = frame_pixels.shape
    weights = interp[0]
    depth, voxels = weights.shape
    own = mirror_pair.shape[1]
    blocks = owner_map.shape[1]
    panels = rows // PANEL_ROWS

    ends = slabs - 1
    top = lax.ppermute(frame_pixels[:, rows - RADIUS :], "slabs", [(i, i + 1) for i in range(ends)])
    bottom = lax.ppermute(frame_pixels[:, :RADIUS], "slabs", [(i + 1, i) for i in range(ends)])

    share = reversed_share(weights, chip, 1 - core, chips, chunks)
    inner = [lax.ppermute(w, "slabs", [(1, 2), (2, 1)]) for w in share]
    inward = [lax.ppermute(w, "slabs", [(0, 1), (3, 2)]) for w in share]

    cuts = [(0, 2), (2, frames - 2)] if frames > 2 else [(0, frames)]
    local = []
    for first, count in cuts:
        local.append(normalize(frame_pixels, bragg_mask, top, bottom, first, count, 2))
    near = [swap(x, "slabs", 1) for x in local]
    beside = [swap(x, "frames", 1) for x in local]
    near_beside = [swap(x, "frames", 1) for x in near]

    through = [lax.ppermute(w, "slabs", [(1, 2), (2, 1)]) for w in inward]
    outward = [lax.ppermute(w, "slabs", [(2, 3), (1, 0)]) for w in inner]
    arrived = [a + b for a, b in zip(through, outward)]

    gathered = []
    if chips == 4:
        share_rows = depth // chips
        cut = share_rows // 2
        for w in arrived:
            a = swap(w, "frames", 2)
            b = swap(w, "frames", 4)
            c = swap(b[:cut], "frames", 2)
            d = swap(a[cut:], "frames", 4)
            gathered.append([w, a, b, c, d])
        offsets = jnp.stack([chip, chip ^ 1, chip ^ 2, chip ^ 3, chip ^ 3]) * share_rows
        offsets = offsets + jnp.array([0, 0, 0, 0, cut])
    else:
        groups = [[i for i in range(members) if i % 2 == c] for c in range(2)]
        for w in arrived:
            gathered.append([lax.all_gather(w, "frames", axis=0, tiled=True, axis_index_groups=groups)])
        offsets = jnp.zeros((1,), jnp.int32)

    listed = block_list[:, 0, :].reshape(frames, slabs, panels).transpose(1, 0, 2).reshape(slabs, frames * panels)
    listed = listed[slab ^ jnp.arange(slabs)].reshape(1, slabs * frames * panels)
    found = positions(listed, owner_map[0], mirror_pair[0])
    n = frames * panels
    other_pos = swap(found[1:2, 2 * n :], "slabs", 2)
    pos = jnp.concatenate([found[0:1, : 2 * n], other_pos], axis=0)
    pos_beside = swap(pos, "frames", 1)
    pos = jnp.concatenate([pos[:, :n], pos_beside[:, :n], pos[:, n:], pos_beside[:, n:]], axis=1)

    own_set = local + beside
    near_set = near + near_beside
    total = own_products(own_set, pos[0:1, : 2 * n], weights, core, blocks, chunks)
    total = own_products(near_set, pos[0:1, 2 * n :], weights, core, blocks, chunks, total)
    owned = []
    other = []
    for j in range(chunks):
        part = partner_products(own_set + near_set, pos[1:2], gathered[j], offsets, total, j)
        width = part.shape[1]
        sent = part.reshape(members, blocks // members, width)
        got = lax.all_to_all(sent, "frames", 0, 0, tiled=True)
        mine = got.reshape(chips, 2, own, width).astype(jnp.float32).sum(axis=0)
        owned.append(mine)
        other.append(swap(mine.astype(jnp.bfloat16), "slabs", 2))
    merged = merge(owned, other, mirror_pair.reshape(own, 1))
    return merged[None]


def solution(mesh):
    return jax.shard_map(
        shards,
        mesh=mesh,
        in_specs=(
            P("frames", "slabs", None),
            P("frames", "slabs", None),
            P("slabs", None, None),
            P("frames", "slabs", None),
            P("slabs", None),
            P("slabs", None),
        ),
        out_specs=P("slabs", "frames", None),
        check_vma=False,
    )
```

```python
import functools

import jax
import jax.numpy as jnp
from jax import lax
from jax.experimental import pallas as pl
from jax.experimental.pallas import tpu as pltpu
from jax.sharding import PartitionSpec as P


PANEL_ROWS = 4
RADIUS = 4
EPSILON = 1e-05
LANES = 128
VMEM_LIMIT = 24 * 1024 * 1024


def swap(cells, axis, bit):
    count = lax.axis_size(axis)
    return lax.ppermute(cells, axis, [(i, i ^ bit) for i in range(count)])


def normalize_kernel(pixel_ref, mask_ref, top_ref, bottom_ref, out_ref, ext, plain, square, parts, flat):
    frames, rows, cols = pixel_ref.shape
    ext_rows = rows + 2 * RADIUS
    area = (2 * RADIUS + 1) ** 2
    tile = 2 * LANES
    parts[:, :LANES] = jnp.zeros((parts.shape[0], LANES), jnp.bfloat16)
    parts[:, LANES + cols :] = jnp.zeros((parts.shape[0], LANES), jnp.bfloat16)
    a = lax.broadcasted_iota(jnp.int32, (2 * tile, tile), 0)
    b = lax.broadcasted_iota(jnp.int32, (2 * tile, tile), 1)
    band = jnp.where(jnp.abs(a - LANES - b) <= RADIUS, 1.0, 0.0).astype(jnp.bfloat16)

    def down(x):
        two = x + pltpu.roll(x, ext_rows - 1, 0)
        four = two + pltpu.roll(two, ext_rows - 2, 0)
        eight = four + pltpu.roll(four, ext_rows - 4, 0)
        return eight[:rows] + x[2 * RADIUS :]

    for f in range(frames):
        ext[0:RADIUS] = top_ref[f]
        ext[RADIUS : RADIUS + rows] = pixel_ref[f]
        ext[RADIUS + rows :] = bottom_ref[f]
        for strip in range(cols // LANES):
            at = slice(strip * LANES, (strip + 1) * LANES)
            to = slice(LANES + strip * LANES, LANES + (strip + 1) * LANES)
            x = ext[:, at]
            for n, total in enumerate((down(x), down(x * x))):
                for k in range(3):
                    term = total.astype(jnp.bfloat16)
                    base = ((f * 2 + n) * 3 + k) * rows
                    parts[base : base + rows, to] = term
                    total = total - term.astype(jnp.float32)
    for j in range(cols // tile):
        sums = jnp.dot(parts[:, j * tile : (j + 2) * tile], band, preferred_element_type=jnp.float32)
        for f in range(frames):
            for n, to in enumerate((plain, square)):
                base = (f * 2 + n) * 3 * rows
                low = sums[base + rows : base + 2 * rows] + sums[base + 2 * rows : base + 3 * rows]
                to[f, :, j * tile : (j + 1) * tile] = sums[base : base + rows] + low
    for f in range(frames):

        def strip_rows(i, carry):
            at = pl.ds(pl.multiple_of(i * 8, 8), 8)
            mean = plain[f, at, :] * (1.0 / area)
            var = jnp.maximum(square[f, at, :] * (1.0 / area) - mean * mean, 0.0)
            scaled = (pixel_ref[f, at, :] - mean) * lax.rsqrt(var + EPSILON)
            kept = jnp.where(mask_ref[f, at, :] == 1, 0.0, scaled)
            to = pl.ds(pl.multiple_of(f * rows + i * 8, 8), 8)
            for strip in range(cols // LANES):
                flat[strip, to, :] = kept[:, strip * LANES : (strip + 1) * LANES]
            return carry

        lax.fori_loop(0, rows // 8, strip_rows, 0, unroll=2)
    panels = frames * rows // PANEL_ROWS
    for r in range(PANEL_ROWS):
        for strip in range(cols // LANES):
            at = r * cols + strip * LANES
            out_ref[:, at : at + LANES] = flat[strip, pl.ds(r, panels, stride=PANEL_ROWS), :].astype(jnp.bfloat16)


def normalize(pixels, mask, top, bottom, first, count, step):
    _, rows, cols = pixels.shape
    block = step * rows // PANEL_ROWS
    base = first // step
    at = lambda i: (base + i, 0, 0)
    return pl.pallas_call(
        normalize_kernel,
        grid=(count // step,),
        in_specs=[
            pl.BlockSpec((step, rows, cols), at),
            pl.BlockSpec((step, rows, cols), at),
            pl.BlockSpec((step, RADIUS, cols), at),
            pl.BlockSpec((step, RADIUS, cols), at),
        ],
        out_specs=pl.BlockSpec((block, PANEL_ROWS * cols), lambda i: (i, 0)),
        out_shape=jax.ShapeDtypeStruct((count * rows // PANEL_ROWS, PANEL_ROWS * cols), jnp.bfloat16),
        scratch_shapes=[
            pltpu.VMEM((rows + 2 * RADIUS, cols), jnp.float32),
            pltpu.VMEM((step, rows, cols), jnp.float32),
            pltpu.VMEM((step, rows, cols), jnp.float32),
            pltpu.VMEM((step * 6 * rows, cols + 2 * LANES), jnp.bfloat16),
            pltpu.VMEM((cols // LANES, step * rows, LANES), jnp.float32),
        ],
        cost_estimate=pl.CostEstimate(flops=60 * count * rows * cols, bytes_accessed=10 * count * rows * cols, transcendentals=count * rows * cols),
        name="normalize",
    )(pixels, mask, top, bottom)


def anti_identity(n):
    a = lax.broadcasted_iota(jnp.int32, (n, n), 0)
    b = lax.broadcasted_iota(jnp.int32, (n, n), 1)
    return jnp.where(a + b == n - 1, 1.0, 0.0).astype(jnp.bfloat16)


def reversed_kernel(at_ref, w_ref, *outs):
    n = len(outs)
    width = outs[0].shape[1]
    flip = anti_identity(width)
    for j, out in enumerate(outs):
        k = n - 1 - j
        out[...] = jnp.dot(w_ref[:, k * width : (k + 1) * width], flip, preferred_element_type=jnp.float32).astype(jnp.bfloat16)


def reversed_share(weights, chip, other, chips, chunks):
    depth, voxels = weights.shape
    rows = depth // chips
    half = voxels // 2
    out = jax.ShapeDtypeStruct((rows, half // chunks), jnp.bfloat16)
    steps = 1
    spec = pl.BlockSpec((rows // steps, half // chunks), lambda i, at: (i, 0))
    return pl.pallas_call(
        reversed_kernel,
        grid_spec=pltpu.PrefetchScalarGridSpec(
            num_scalar_prefetch=1,
            grid=(steps,),
            in_specs=[pl.BlockSpec((rows // steps, half), lambda i, at: (at[0] * steps + i, at[1]))],
            out_specs=[spec] * chunks,
        ),
        out_shape=[out] * chunks,
        cost_estimate=pl.CostEstimate(flops=rows * half * half, bytes_accessed=4 * rows * half, transcendentals=0),
        name="reversed_share",
    )(jnp.stack([chip, other]).astype(jnp.int32), weights)


def position_kernel(panels, at_ref, list_ref, table_ref, mirror_ref, out_ref):
    frames, _, listed = list_ref.shape
    slabs = listed // panels
    blocks = table_ref.shape[1]
    own = mirror_ref.shape[1]
    shift = own.bit_length() - 1
    entries = frames * listed
    as_bf16 = lambda x: x.astype(jnp.float32).astype(jnp.bfloat16)
    hot_of = lambda row, n: as_bf16(lax.broadcasted_iota(jnp.int32, (n, row.shape[1]), 0) == row)
    dot = functools.partial(jnp.dot, preferred_element_type=jnp.float32)
    row_at = lax.broadcasted_iota(jnp.int32, (8, blocks), 0)
    table = as_bf16(jnp.where(row_at == 0, table_ref[...] >> shift, table_ref[...] & (own - 1)))
    mirror = as_bf16(jnp.broadcast_to(mirror_ref[...], (8, own)))
    found = jnp.zeros((8, frames * panels * slabs), jnp.float32)
    target = lax.broadcasted_iota(jnp.int32, (listed, entries), 1)
    source = lax.broadcasted_iota(jnp.int32, (listed, entries), 0)
    run = frames * panels
    plane = sum([(target >= q * run).astype(jnp.int32) for q in range(1, slabs)])
    rest = target - plane * run
    frame = sum([(rest >= f * panels).astype(jnp.int32) for f in range(1, frames)])
    want = (plane ^ at_ref[0]) * panels + rest - frame * panels
    for f in range(frames):
        here = dot(table, hot_of(list_ref[f], blocks))
        pick = as_bf16((source == want) & (frame == f))
        found = found + dot(here.astype(jnp.bfloat16), pick)
    found = found.astype(jnp.int32)
    owner = found[0:1]
    slot = found[1:2]
    mirrored = dot(mirror, hot_of(slot, own)).astype(jnp.int32)
    out_ref[0:1] = owner * own + slot
    out_ref[1:2] = owner * own + mirrored[0:1]


def positions(block_list, owner_map, mirror_pair, panels, slab):
    frames, _, listed = block_list.shape
    whole = pl.BlockSpec(memory_space=pltpu.VMEM)
    return pl.pallas_call(
        functools.partial(position_kernel, panels),
        in_specs=[pl.BlockSpec(memory_space=pltpu.SMEM), whole, whole, whole],
        out_shape=jax.ShapeDtypeStruct((2, frames * listed), jnp.int32),
        compiler_params=pltpu.CompilerParams(vmem_limit_bytes=VMEM_LIMIT),
        name="positions",
    )(slab[None].astype(jnp.int32), block_list, owner_map, mirror_pair)


def add_rows(pos, product, blocks):
    hot = (lax.broadcasted_iota(jnp.int32, (blocks, pos.shape[1]), 0) == pos).astype(jnp.float32).astype(jnp.bfloat16)
    high = product.astype(jnp.bfloat16)
    low = (product - high.astype(jnp.float32)).astype(jnp.bfloat16)
    return jnp.dot(hot, high, preferred_element_type=jnp.float32) + jnp.dot(hot, low, preferred_element_type=jnp.float32)


def own_kernel(xs_count, half_ref, *refs):
    xs = refs[:xs_count]
    w_ref, pos_ref = refs[xs_count : xs_count + 2]
    outs = refs[xs_count + 2 : -3]
    w_buf, product, sem = refs[-3:]
    blocks, width = outs[0].shape
    copies = []
    for j in range(len(outs)):
        lane = pl.multiple_of((half_ref[0] * len(outs) + j) * width, LANES)
        copies.append(pltpu.make_async_copy(w_ref.at[:, pl.ds(lane, width)], w_buf.at[j], sem.at[j]))
        copies[-1].start()
    for j, out in enumerate(outs):
        copies[j].wait()
        row = 0
        for x in xs:
            n = x.shape[0]
            product[row : row + n] = jnp.dot(x[...], w_buf[j], preferred_element_type=jnp.float32)
            row += n
        out[...] = add_rows(pos_ref[...], product[...], blocks)


def own_products(xs, pos, weights, core, blocks, chunks):
    depth, voxels = weights.shape
    width = voxels // 2 // chunks
    rows = sum(x.shape[0] for x in xs)
    whole = pl.BlockSpec(memory_space=pltpu.VMEM)
    return pl.pallas_call(
        functools.partial(own_kernel, len(xs)),
        in_specs=[pl.BlockSpec(memory_space=pltpu.SMEM)] + [whole] * len(xs) + [pl.BlockSpec(memory_space=pltpu.HBM), whole],
        out_specs=[whole] * chunks,
        out_shape=[jax.ShapeDtypeStruct((blocks, width), jnp.float32)] * chunks,
        scratch_shapes=[
            pltpu.VMEM((chunks, depth, width), jnp.bfloat16),
            pltpu.VMEM((rows, width), jnp.float32),
            pltpu.SemaphoreType.DMA((chunks,)),
        ],
        compiler_params=pltpu.CompilerParams(vmem_limit_bytes=56 * 1024 * 1024),
        cost_estimate=pl.CostEstimate(flops=2 * rows * chunks * width * (depth + 2 * blocks), bytes_accessed=2 * depth * (rows + voxels // 2) + 4 * blocks * voxels // 2, transcendentals=0),
        name="own_products",
    )(core[None].astype(jnp.int32), *xs, weights, pos)


def last_kernel(far, xs_count, pieces, chunks, chunk, at_ref, *refs):
    xs = refs[:xs_count]
    ws = refs[xs_count : xs_count + pieces]
    w_ref, pos_ref, before_ref, out_ref, w_buf, product, sem = refs[xs_count + pieces :]
    blocks, width = out_ref.shape
    lane = pl.multiple_of((at_ref[0] * chunks + chunk) * width, LANES)
    copy = pltpu.make_async_copy(w_ref.at[:, pl.ds(lane, width)], w_buf, sem)
    copy.start()
    row = 0
    for x in xs:
        n = x.shape[0]
        acc = None
        for k, w in enumerate(ws):
            at = pl.ds(pl.multiple_of(at_ref[1 + k], LANES), w.shape[0])
            term = jnp.dot(x[:, at], w[...], preferred_element_type=jnp.float32)
            acc = term if acc is None else acc + term
        product[row : row + n] = acc
        row += n
    copy.wait()
    for x in xs[far:]:
        n = x.shape[0]
        product[row : row + n] = jnp.dot(x[...], w_buf[...], preferred_element_type=jnp.float32)
        row += n
    total = add_rows(pos_ref[...], product[...], blocks) + before_ref[...]
    out_ref[...] = (0.5 * total).astype(jnp.bfloat16)


def last_products(xs, far, pos, pieces, offsets, weights, core, before, chunks, chunk):
    depth = weights.shape[0]
    blocks, width = before.shape
    rows = pos.shape[1]
    whole = pl.BlockSpec(memory_space=pltpu.VMEM)
    return pl.pallas_call(
        functools.partial(last_kernel, far, len(xs), len(pieces), chunks, chunk),
        in_specs=[pl.BlockSpec(memory_space=pltpu.SMEM)] + [whole] * (len(xs) + len(pieces)) + [pl.BlockSpec(memory_space=pltpu.HBM), whole, whole],
        out_specs=whole,
        out_shape=jax.ShapeDtypeStruct((blocks, width), jnp.bfloat16),
        scratch_shapes=[
            pltpu.VMEM((depth, width), jnp.bfloat16),
            pltpu.VMEM((rows, width), jnp.float32),
            pltpu.SemaphoreType.DMA,
        ],
        compiler_params=pltpu.CompilerParams(vmem_limit_bytes=52 * 1024 * 1024),
        cost_estimate=pl.CostEstimate(flops=2 * rows * width * (depth + 2 * blocks), bytes_accessed=2 * depth * (rows + 2 * width) + 6 * blocks * width, transcendentals=0),
        name="last_products",
    )(jnp.concatenate([core[None], offsets]).astype(jnp.int32), *xs, *pieces, weights, pos, before)


def merge_kernel(chunks, mirror_ref, *refs):
    owned = refs[:chunks]
    other = refs[chunks : 2 * chunks]
    out_ref = refs[-1]
    _, rows, width = owned[0].shape
    half = width * chunks
    flip = anti_identity(width)
    pick = (lax.broadcasted_iota(jnp.int32, (rows, rows), 1) == mirror_ref[...]).astype(jnp.float32).astype(jnp.bfloat16)
    for h in range(2):
        for j in range(chunks):
            turned = jnp.dot(other[chunks - 1 - j][1 - h], flip, preferred_element_type=jnp.float32).astype(jnp.bfloat16)
            paired = jnp.dot(pick, turned, preferred_element_type=jnp.float32)
            at = h * half + j * width
            out_ref[:, at : at + width] = owned[j][h] + paired


def merge(owned, other, mirror_col):
    _, rows, width = owned[0].shape
    return pl.pallas_call(
        functools.partial(merge_kernel, len(owned)),
        out_shape=jax.ShapeDtypeStruct((rows, 2 * width * len(owned)), jnp.float32),
        compiler_params=pltpu.CompilerParams(vmem_limit_bytes=VMEM_LIMIT),
        name="merge",
    )(mirror_col, *owned, *other)


def shards(frame_pixels, bragg_mask, interp, block_list, owner_map, mirror_pair):
    slab = lax.axis_index("slabs")
    member = lax.axis_index("frames")
    members = lax.axis_size("frames")
    slabs = lax.axis_size("slabs")
    assert slabs == 4 and members % 2 == 0
    chips = members // 2
    core = member & 1
    chip = member >> 1
    chunks = 2
    frames, rows, _ = frame_pixels.shape
    weights = interp[0]
    depth, _ = weights.shape
    own = mirror_pair.shape[1]
    blocks = owner_map.shape[1]
    panels = rows // PANEL_ROWS

    ends = slabs - 1
    top = lax.ppermute(frame_pixels[:, rows - RADIUS :], "slabs", [(i, i + 1) for i in range(ends)])
    bottom = lax.ppermute(frame_pixels[:, :RADIUS], "slabs", [(i + 1, i) for i in range(ends)])

    share = reversed_share(weights, chip, 1 - core, chips, chunks)
    arrived = []
    for w in share:
        up = lax.ppermute(w, "slabs", [(0, 1), (1, 2)])
        down = lax.ppermute(w, "slabs", [(3, 2), (2, 1)])
        up = lax.ppermute(up, "slabs", [(1, 2), (2, 3)])
        down = lax.ppermute(down, "slabs", [(2, 1), (1, 0)])
        arrived.append(up + down)

    cuts = [(0, 2), (2, frames - 2)] if frames > 2 else [(0, frames)]
    local, near, beside, near_beside = [], [], [], []
    for i, (first, count) in enumerate(cuts):
        x = normalize(frame_pixels, bragg_mask, top, bottom, first, count, 2)
        local.append(x)
        near.append(swap(x, "slabs", 1))
        beside.append(swap(x, "frames", 1))
        near_beside.append(swap(near[i], "frames", 1))

    gathered = []
    if chips == 4:
        share_rows = depth // chips
        for j, w in enumerate(arrived):
            a = swap(w, "frames", 2)
            b = swap(w, "frames", 4)
            c = swap(b, "frames", 2) if j % 2 == 0 else swap(a, "frames", 4)
            gathered.append([w, a, b, c])
        offsets = (chip ^ jnp.arange(4)) * share_rows
    else:
        groups = [[i for i in range(members) if i % 2 == c] for c in range(2)]
        for w in arrived:
            gathered.append([lax.all_gather(w, "frames", axis=0, tiled=True, axis_index_groups=groups)])
        offsets = jnp.zeros((1,), jnp.int32)

    found = positions(block_list, owner_map, mirror_pair, panels, slab)
    n = frames * panels
    partner = swap(found[1:2, 2 * n :], "slabs", 2)
    own_beside = swap(found[0:1, : 2 * n], "frames", 1)
    partner_beside = swap(partner, "frames", 1)
    mine = found[0:1]
    own_early = jnp.concatenate([mine[:, :n], own_beside[:, :n]], axis=1)
    late_pos = jnp.concatenate(
        [partner[:, :n], partner_beside[:, :n], partner[:, n:], partner_beside[:, n:], mine[:, n : 2 * n], own_beside[:, n:]], axis=1
    )

    own_set = local + beside
    near_set = near + near_beside
    totals = own_products(own_set, own_early, weights, core, blocks, chunks)
    owned = []
    other = []
    for j in range(chunks):
        part = last_products(own_set + near_set, len(own_set), late_pos, gathered[j], offsets, weights, core, totals[j], chunks, j)
        width = part.shape[1]
        sent = part.reshape(members, blocks // members, width)
        got = lax.all_to_all(sent, "frames", 0, 0, tiled=True)
        mine = got.reshape(chips, 2, own, width).astype(jnp.float32).sum(axis=0)
        owned.append(mine)
        other.append(swap(mine.astype(jnp.bfloat16), "slabs", 2))
    merged = merge(owned, other, mirror_pair.reshape(own, 1))
    return merged[None]


def solution(mesh):
    return jax.shard_map(
        shards,
        mesh=mesh,
        in_specs=(
            P("frames", "slabs", None),
            P("frames", "slabs", None),
            P("slabs", None, None),
            P("frames", "slabs", None),
            P("slabs", None),
            P("slabs", None),
        ),
        out_specs=P("slabs", "frames", None),
        check_vma=False,
    )
```
